32 devices in a mesh: row: 4 (over y, x), col: 8 (over z, core).
Axes of the slice: x: 2, y: 2, z: 4, core: 2. Of those that a mesh axis runs over, the one named last changes fastest.
Arguments:
- coeffs: bfloat16 [16384, 2048], P('row'), may hold values from -1 to 1
- p_slots: int32 [4, 8, 64], P('row', 'col'), may hold values from 0 to 511, as said below
- p_count: int32 [4, 8], P('row', 'col'), may hold values from 1 to 64
- s_blocks: bfloat16 [4, 8, 64, 128, 128], P('row', 'col'), may hold values from -0.3984375 to 0.3984375
- s_slots: int32 [4, 8, 64], P('row', 'col'), may hold values from 0 to 511, as said below
- s_count: int32 [4, 8], P('row', 'col'), may hold values from 1 to 64
- q_slots: int32 [4, 8, 64], P('row', 'col'), may hold values from 0 to 511, as said below
- q_count: int32 [4, 8], P('row', 'col'), may hold values from 1 to 64
Outputs:
- density: bfloat16 [4, 8, 64, 128, 128], P('row', 'col')
- product: float32 [4, 8, 64, 128, 128], P('row', 'col')
The draws below stay inside these ranges and needn't reach their ends.
Inputs may be any that keep to these rules, and one draw needn't show every extreme that they name: `p_slots`: on each device the live slots name different blocks of its tile; at least one device has all 64 slots live, which one is drawn. `s_slots`: on each device the live slots name different positions; at least one device has all 64 slots live, which one is drawn. `q_slots`: on each device the live slots name different blocks of its tile; at least one device has all 64 slots live, which one is drawn.
All inputs are finite; a program needn't handle non-finite values.
Results may differ from the reference program's by a relative error of at most 0.0029.
Values may be sent and summed in bfloat16 or wider, within the bound.
No kernel may reach another device: no remote copies, remote signals or barrier semaphores. Data moves between devices by JAX's collectives and lax.ppermute only.
A program may use at most 192 MiB of HBM per device.

```python
import jax
import jax.numpy as jnp
from jax import lax

N = 16384
K = 2048
ROWB = 32
COLB = 16
SPAN = 2
PMAX = 64
QMAX = 64
SMAX = 64
N_ROW = 4
N_COL = 8


def pattern_slots(key, total, most):
    keys = jax.random.split(key, N_ROW * N_COL)
    picks = jax.vmap(lambda single: jax.random.permutation(single, total)[:most])(keys)
    return picks.reshape(N_ROW, N_COL, most).astype(jnp.int32)


def pattern_count(key, most):
    first_key, second_key = jax.random.split(key)
    counts = jax.random.randint(first_key, (N_ROW * N_COL,), 1, most + 1)
    chosen = jax.random.randint(second_key, (), 0, N_ROW * N_COL)
    counts = jnp.where(jnp.arange(N_ROW * N_COL) == chosen, most, counts)
    return counts.reshape(N_ROW, N_COL).astype(jnp.int32)


def draw_p_slots(key, part):
    return pattern_slots(jax.random.fold_in(key, 11), ROWB * COLB, PMAX)


def draw_p_count(key, part):
    return pattern_count(jax.random.fold_in(key, 12), PMAX)


def draw_s_slots(key, part):
    return pattern_slots(jax.random.fold_in(key, 21), SPAN * COLB * COLB, SMAX)


def draw_s_count(key, part):
    return pattern_count(jax.random.fold_in(key, 22), SMAX)


def draw_q_slots(key, part):
    return pattern_slots(jax.random.fold_in(key, 31), ROWB * COLB, QMAX)


def draw_q_count(key, part):
    return pattern_count(jax.random.fold_in(key, 32), QMAX)


def level_of(stream_key, shape, cuts, low, largest):
    def one(dim, blocks):
        steps = jax.random.uniform(jax.random.fold_in(jax.random.fold_in(stream_key, 6), dim), (blocks,), jnp.float32, low / len(cuts), largest / len(cuts))
        return jnp.repeat(jnp.exp(steps), shape[dim] // blocks).reshape((-1,) + (1,) * (len(shape) - dim - 1))

    gain = one(*cuts[0])
    for cut in cuts[1:]:
        gain = gain * one(*cut)
    return gain


def gaussian(own_key, extent, deviation, limit, shards=(), kind=jnp.bfloat16):
    array = jax.random.normal(own_key, extent, jnp.float32) * deviation
    if len(shards) > 0:
        array = level_of(own_key, extent, shards, -0.22, 0.18) * array
    return jnp.clip(array, min=-limit, max=limit).astype(kind)


def setup_inputs(seed: int = 0) -> dict:
    key_list = jax.random.split(jax.random.key(seed), 9)
    return {
        "coeffs": gaussian(key_list[0], (N, K), 0.15, 1.0, ((0, 4),)),
        "p_slots": draw_p_slots(jax.random.fold_in(key_list[8], 71), 0),
        "p_count": draw_p_count(jax.random.fold_in(key_list[8], 71), 0),
        "s_blocks": gaussian(key_list[3], (N_ROW, N_COL, SMAX, 128, 128), 0.0625, 0.3984375, ((0, 4), (1, 8))),
        "s_slots": draw_s_slots(jax.random.fold_in(key_list[8], 71), 0),
        "s_count": draw_s_count(jax.random.fold_in(key_list[8], 71), 0),
        "q_slots": draw_q_slots(jax.random.fold_in(key_list[8], 71), 0),
        "q_count": draw_q_count(jax.random.fold_in(key_list[8], 71), 0),
    }


def reference(coeffs, p_slots, p_count, s_blocks, s_slots, s_count, q_slots, q_count):
    block_count = coeffs.shape[0] // 128
    orbitals = coeffs.shape[1]
    tile_rows = block_count // N_ROW
    tile_cols = block_count // N_COL
    grid_row = jnp.arange(N_ROW, dtype=jnp.int32)[:, None, None]
    grid_col = jnp.arange(N_COL, dtype=jnp.int32)[None, :, None]
    blocked = coeffs.reshape(block_count, 128, orbitals)

    p_live = jnp.arange(p_slots.shape[2], dtype=jnp.int32)[None, None, :] < p_count[:, :, None]
    p_global_row = (grid_row * tile_rows + p_slots // tile_cols).astype(jnp.int32).reshape(-1)
    p_global_col = (grid_col * tile_cols + p_slots % tile_cols).astype(jnp.int32).reshape(-1)

    def density_block(pair):
        return jnp.dot(blocked[pair[0]], blocked[pair[1]].T, preferred_element_type=jnp.float32)

    raw = lax.map(density_block, (p_global_row, p_global_col))
    raw = raw.reshape(N_ROW, N_COL, -1, 128, 128)
    density = jnp.where(p_live[..., None, None], raw, jnp.zeros_like(raw)).astype(jnp.bfloat16)

    dense_p = jnp.zeros((block_count, block_count, 128, 128), jnp.bfloat16)
    dense_p = dense_p.at[p_global_row, p_global_col].add(density.reshape(-1, 128, 128))

    s_live = jnp.arange(s_slots.shape[2], dtype=jnp.int32)[None, None, :] < s_count[:, :, None]
    local_row = s_slots // tile_cols
    panel_index = grid_row + N_ROW * (local_row // tile_cols)
    s_global_row = (panel_index * tile_cols + local_row % tile_cols).astype(jnp.int32).reshape(-1)
    s_global_col = (grid_col * tile_cols + s_slots % tile_cols).astype(jnp.int32).reshape(-1)
    s_kept = jnp.where(s_live[..., None, None], s_blocks, jnp.zeros_like(s_blocks)).reshape(-1, 128, 128)
    dense_s = jnp.zeros((block_count, block_count, 128, 128), jnp.bfloat16)
    dense_s = dense_s.at[s_global_row, s_global_col].add(s_kept)

    q_live = jnp.arange(q_slots.shape[2], dtype=jnp.int32)[None, None, :] < q_count[:, :, None]
    q_global_row = (grid_row * tile_rows + q_slots // tile_cols).astype(jnp.int32).reshape(-1)
    q_global_col = (grid_col * tile_cols + q_slots % tile_cols).astype(jnp.int32).reshape(-1)

    def product_block(pair):
        left = dense_p[pair[0]].astype(jnp.float32)
        right = dense_s[:, pair[1]].astype(jnp.float32)
        return jnp.einsum('kab,kbc->ac', left, right)

    summed = lax.map(product_block, (q_global_row, q_global_col))
    summed = summed.reshape(N_ROW, N_COL, -1, 128, 128)
    product = jnp.where(q_live[..., None, None], summed, jnp.zeros_like(summed))
    return density, product
```

```python
import jax
import jax.numpy as jnp
from jax import lax
from jax.experimental import pallas as pl
from jax.experimental.pallas import tpu as pltpu
from jax.sharding import PartitionSpec as P

VMEM_LIMIT = 58 * 1024 * 1024


def density_kernel(count_ref, row_ref, col_ref, left_ref, right_ref, out_ref):
    count = count_ref[0]

    def compute(slot, carry):
        out_ref[slot] = lax.dot_general(
            left_ref[row_ref[slot]],
            right_ref[col_ref[slot]],
            (((1,), (1,)), ((), ())),
            preferred_element_type=jnp.float32,
        ).astype(out_ref.dtype)
        return carry

    def clear(slot, carry):
        out_ref[slot] = jnp.zeros(out_ref.shape[1:], out_ref.dtype)
        return carry

    lax.fori_loop(0, count, compute, 0)
    lax.fori_loop(count, out_ref.shape[0], clear, 0)


def density_blocks(count, rows, cols, left, right):
    smem = pl.BlockSpec(memory_space=pltpu.SMEM)
    vmem = pl.BlockSpec(memory_space=pltpu.VMEM)
    return pl.pallas_call(
        density_kernel,
        out_shape=jax.ShapeDtypeStruct((rows.shape[0], 128, 128), jnp.bfloat16),
        in_specs=[smem, smem, smem, vmem, vmem],
        out_specs=vmem,
        compiler_params=pltpu.CompilerParams(vmem_limit_bytes=VMEM_LIMIT),
        name="density_blocks",
    )(count, rows, cols, left, right)


EAGER = 2


def product_kernel(count_ref, left_at, right_at, p_hbm, *rest):
    parts = len(rest) - 4
    s_hbm = rest[:parts]
    out_ref, p_ref, s_ref, sems = rest[parts:]
    s_max = s_ref.shape[0] // parts
    copies = [pltpu.make_async_copy(p_hbm, p_ref, sems.at[parts])]
    for d in range(parts):
        copies.append(
            pltpu.make_async_copy(s_hbm[d], s_ref.at[pl.ds(d * s_max, s_max)], sems.at[d])
        )
    for copy in copies:
        copy.start()
    for copy in copies:
        copy.wait()

    def pair(q, n):
        return jnp.dot(
            p_ref[left_at[q, n]], s_ref[right_at[q, n]], preferred_element_type=jnp.float32
        )

    def eager(q, carry):
        count = count_ref[q]
        total = jnp.zeros(out_ref.shape[1:], jnp.float32)
        for n in range(EAGER):
            total = total + jnp.where(n < count, pair(q, n), 0.0)
        out_ref[q] = total
        return carry

    def rest_of(q, carry):
        def add(n, inner):
            out_ref[q] += pair(q, n)
            return inner

        return lax.fori_loop(EAGER, count_ref[q], add, carry)

    lax.fori_loop(0, out_ref.shape[0], eager, 0, unroll=4)
    lax.fori_loop(0, out_ref.shape[0], rest_of, 0)


def product_blocks(counts, left_at, right_at, p_all, s_parts):
    smem = pl.BlockSpec(memory_space=pltpu.SMEM)
    hbm = pl.BlockSpec(memory_space=pl.ANY)
    parts = len(s_parts)
    s_max = s_parts[0].shape[0]
    return pl.pallas_call(
        product_kernel,
        out_shape=jax.ShapeDtypeStruct((counts.shape[0], 128, 128), jnp.float32),
        in_specs=[smem, smem, smem, hbm] + [hbm] * parts,
        out_specs=pl.BlockSpec(memory_space=pltpu.VMEM),
        scratch_shapes=[
            pltpu.VMEM(p_all.shape, p_all.dtype),
            pltpu.VMEM((parts * s_max, 128, 128), s_parts[0].dtype),
            pltpu.SemaphoreType.DMA((parts + 1,)),
        ],
        compiler_params=pltpu.CompilerParams(vmem_limit_bytes=VMEM_LIMIT),
        name="product_blocks",
    )(counts, left_at, right_at, p_all, *s_parts)


def exact_dot(left, right):
    return jnp.dot(
        left.astype(jnp.float32),
        right.astype(jnp.float32),
        precision=lax.Precision.HIGHEST,
        preferred_element_type=jnp.float32,
    )


def found_at(mine, theirs, live, place, inner, inner_count):
    hit = (mine[:, None] == theirs[None, :]) & live[None, :]
    weight = jnp.where(hit, place[None, :] + 1, 0)
    at = inner[:, None] == jnp.arange(inner_count, dtype=jnp.int32)[None, :]
    return exact_dot(weight, at)


def on_device(coeffs, p_slots, p_count, s_blocks, s_slots, s_count, q_slots, q_count):
    rows_n = lax.axis_size("row")
    cols_n = lax.axis_size("col")
    row_at = lax.axis_index("row")
    col_at = lax.axis_index("col")
    panel_rows, orbitals = coeffs.shape
    tile_rows = panel_rows // 128
    tile_cols = panel_rows * rows_n // cols_n // 128
    span = cols_n // rows_n
    k_count = cols_n * tile_cols

    piece = tile_cols * 128 // rows_n
    start = col_at % span * (tile_cols * 128) + col_at // span * piece
    route = []
    for r in range(rows_n):
        for c in range(cols_n):
            to = (c // span) * cols_n + r * span + c % span
            route.append((r * cols_n + c, to))
    sent = lax.dynamic_slice_in_dim(coeffs, start, piece, 0)
    got = lax.ppermute(sent, ("row", "col"), route)
    column_rows = lax.all_gather(got, "row", axis=0, tiled=True)

    p_ids = p_slots[0, 0]
    p_max = p_ids.shape[0]
    p_code = jnp.where(jnp.arange(p_max, dtype=jnp.int32) < p_count[0, 0], p_ids, -1)
    s_ids = s_slots[0, 0]
    s_max = s_ids.shape[0]
    s_code = jnp.where(jnp.arange(s_max, dtype=jnp.int32) < s_count[0, 0], s_ids, -1)
    q_ids = q_slots[0, 0]
    q_max = q_ids.shape[0]
    q_live = jnp.arange(q_max, dtype=jnp.int32) < q_count[0, 0]
    q_row = q_ids // tile_cols
    q_col = q_ids % tile_cols

    p_codes = lax.all_gather(p_code, "col").reshape(-1)
    s_codes = lax.all_gather(s_code, "row").reshape(-1)
    p_place = jnp.arange(cols_n * p_max, dtype=jnp.int32)
    p_live = p_codes >= 0
    p_local = jnp.maximum(p_codes, 0)
    p_k = p_place // p_max * tile_cols + p_local % tile_cols
    p_found = found_at(q_row, p_local // tile_cols, p_live, p_place, p_k, k_count)
    s_order = jnp.arange(rows_n * s_max, dtype=jnp.int32)
    s_from = s_order // s_max
    s_place = (row_at - s_from + rows_n) % rows_n * s_max + s_order % s_max
    s_live = s_codes >= 0
    s_local = jnp.maximum(s_codes, 0)
    local_row = s_local // tile_cols
    s_k = (s_from + rows_n * (local_row // tile_cols)) * tile_cols + local_row % tile_cols
    s_found = found_at(q_col, s_local % tile_cols, s_live, s_place, s_k, k_count)
    match = (p_found > 0) & (s_found > 0) & q_live[:, None]
    steps = jnp.arange(k_count, dtype=jnp.int32)
    rank = exact_dot(match, steps[:, None] < steps[None, :]).astype(jnp.int32)
    code = (p_found.astype(jnp.int32) - 1) * (rows_n * s_max) + s_found.astype(jnp.int32) - 1
    chosen = match[:, None, :] & (rank[:, None, :] == steps[None, :, None])
    listed = jnp.sum(jnp.where(chosen, code[:, None, :], 0), axis=2, dtype=jnp.int32)
    counts = jnp.sum(match, axis=1, dtype=jnp.int32)
    left_at = listed // (rows_n * s_max)
    right_at = listed % (rows_n * s_max)

    dense = density_blocks(
        p_count[0],
        p_ids // tile_cols,
        p_ids % tile_cols,
        coeffs.reshape(tile_rows, 128, orbitals),
        column_rows.reshape(tile_cols, 128, orbitals),
    )
    p_all = lax.all_gather(dense, "col", axis=0, tiled=True)
    s_own, _ = lax.optimization_barrier((s_blocks[0, 0], dense))
    s_parts = [s_own]
    for d in range(1, rows_n):
        s_parts.append(lax.ppermute(s_own, "row", [(i, (i + d) % rows_n) for i in range(rows_n)]))
    product = product_blocks(counts, left_at, right_at, p_all, s_parts)
    return (dense.reshape(1, 1, p_max, 128, 128), product.reshape(1, 1, q_max, 128, 128))


def solution(mesh):
    return jax.shard_map(
        on_device,
        mesh=mesh,
        in_specs=(
            P("row", None),
            P("row", "col", None),
            P("row", "col"),
            P("row", "col", None, None, None),
            P("row", "col", None),
            P("row", "col"),
            P("row", "col", None),
            P("row", "col"),
        ),
        out_specs=(P("row", "col", None, None, None), P("row", "col", None, None, None)),
        check_vma=False,
    )
```
